256 devices in a mesh: patch: 16 (over z_hi, x), wrow: 4 (over z_lo, core), wcol: 4 (over y).
Axes of the slice: x: 4, y: 4, z: 8 (z_hi: 4, z_lo: 2; z = z_hi * 2 + z_lo), core: 2. Of those that a mesh axis runs over, the one named last changes fastest.
Arguments:
- hidden_states: bfloat16 [4, 8192, 1536], P('wrow', ('patch', 'wcol')), may hold values from -6 to 6
- modulation: float32 [4, 3, 1536], P('wrow'), may hold values from -4 to 4
- w_qkv: bfloat16 [1536, 3, 1536], P('wrow', None, 'wcol'), may hold values from -1 to 1
- w_out: bfloat16 [1536, 1536], P('wcol', 'wrow'), may hold values from -0.15625 to 0.15625
- lengths: int32 [4], P('wrow'), may hold values from 1 to 8192, 20480 in all
Outputs:
- updated: bfloat16 [4, 8192, 1536], P('wrow', ('patch', 'wcol'))
The draws below stay inside these ranges and needn't reach their ends.
Inputs may be any that keep to these rules, and one draw needn't show every extreme that they name: lengths[v] real tokens in video v, padding after them; the longest video fills all 8192 slots.
All inputs are finite; a program needn't handle non-finite values. No bound on the sum of `lengths` on one device may be relied on, other than what follows from the above.
Results may differ from the reference program's by a relative error of at most 0.015.
The reference program's roundings to bfloat16 on the way count: a program that leaves them out, or rounds other values in their place, can miss the bound.
Values may be sent and summed in bfloat16 or wider, within the bound.
A program may use at most 64 MiB of HBM per device.

```python
import math
import jax
import jax.numpy as jnp
import numpy as np
from jax import lax

D = 1536
HEADS = 12
HD = 128
SEQ = 8192
VIDEOS = 4


def draw_w_qkv(key, part):
    key_query, key_key, key_value = jax.random.split(key, 3)
    base = D ** (-0.5)
    query_w = jax.random.normal(key_query, (D, D), jnp.float32) * base
    key_w = jax.random.normal(key_key, (D, D), jnp.float32) * base
    value_w = jax.random.normal(key_value, (D, D), jnp.float32) * base
    stacked = jnp.stack([query_w, key_w, value_w], axis=1)
    return jnp.clip(stacked, -1.0, 1.0).astype(jnp.bfloat16)


def block_scale(own_key, dims, pieces, least, top_value):
    def one(position, blocks):
        steps = jax.random.uniform(jax.random.fold_in(jax.random.fold_in(own_key, 6), position), (blocks,), jnp.float32, least / len(pieces), top_value / len(pieces))
        return jnp.repeat(jnp.exp(steps), dims[position] // blocks).reshape((-1,) + (1,) * (len(dims) - position - 1))

    gain = one(*pieces[0])
    for cut in pieces[1:]:
        gain = gain * one(*cut)
    return gain


def split_up(number_of, total, most, slope):
    loads = [(1 << 20) // math.isqrt(rank ** slope) + 1 for rank in range(2, number_of + 1)]
    spare, given = total - most - (number_of - 1), [1] * (number_of - 1)
    while spare > 0:
        movable = [i for i in range(number_of - 1) if given[i] < most]
        whole, remaining = sum([loads[i] for i in movable]), spare
        for i in movable:
            extra = min(most - given[i], max(1, remaining * loads[i] // whole), spare)
            given[i] = given[i] + extra
            spare = spare - extra
    return np.array([most] + given)


def uneven(key, number_of, total, most, lean):
    if number_of == 2:
        one = jax.random.randint(key, (), max(1, total - most), min(most, total - 1) + 1)
        return jnp.stack([one, total - one])
    tallies = jnp.asarray(split_up(number_of, total, most, lean), jnp.int32)
    couples = (number_of - 1) // 2
    giver, sink = tallies[1:1 + 2 * couples:2], tallies[2:2 + 2 * couples:2]
    room = jnp.minimum(giver - 1, most - sink)
    passed = jax.random.randint(jax.random.fold_in(key, 1), (couples,), 0, 1 << 20) % (room + 1)
    tallies = tallies.at[1:1 + 2 * couples:2].set(giver - passed).at[2:2 + 2 * couples:2].set(sink + passed)
    return tallies[jax.random.permutation(jax.random.fold_in(key, 2), number_of)]


def gaussian(rng, dims, scale, most, cuts=(), held_as=jnp.bfloat16):
    result = scale * jax.random.normal(rng, dims, jnp.float32)
    if cuts:
        result = result * block_scale(rng, dims, cuts, -0.22, 0.18)
    return jnp.clip(result, -most, most).astype(held_as)


def setup_inputs(seed: int = 0) -> dict:
    seeds = jax.random.split(jax.random.key(seed), 6)
    hidden_states = gaussian(seeds[0], (VIDEOS, SEQ, D), 1.0, 6.0, ((0, 4), (1, 64)))
    modulation = gaussian(seeds[1], (VIDEOS, 3, D), 1.0, 4.0, ((0, 4),), jnp.float32)
    w_qkv = draw_w_qkv(jax.random.fold_in(seeds[5], 71), 0)
    w_out = gaussian(seeds[3], (D, D), D ** -0.5, 0.15625, ((0, 4), (1, 4)))
    lengths = uneven(seeds[4], VIDEOS, VIDEOS * SEQ * 5 // 8, SEQ, 2).astype(jnp.int32)
    return dict(hidden_states=hidden_states, modulation=modulation, w_qkv=w_qkv, w_out=w_out, lengths=lengths)


EPSILON = 1e-06
FLOOR = -1e+30

def modulated_norm(states, shift, scale):
    values = states.astype(jnp.float32)
    center = lax.optimization_barrier(jnp.mean(values, axis=-1, keepdims=True))
    spread = lax.optimization_barrier(jnp.mean(jnp.square(values - center), axis=-1, keepdims=True))
    return ((values - center) * lax.rsqrt(spread + EPSILON) * (1.0 + scale) + shift).astype(jnp.bfloat16)

def reference(hidden_states, modulation, w_qkv, w_out, lengths):
    shift = modulation[:, 0][:, None, :]
    scale = modulation[:, 1][:, None, :]
    gate = modulation[:, 2][:, None, :]
    normed = modulated_norm(hidden_states, shift, scale)
    mixed = jnp.dot(normed.reshape(VIDEOS * SEQ, D), w_qkv.reshape(D, 3 * D), preferred_element_type=jnp.float32)
    mixed = mixed.astype(jnp.bfloat16).reshape(VIDEOS, SEQ, 3, HEADS, HD)
    block_rows = math.gcd(SEQ, 512)

    def one_video(items):
        queries, keys, values, limit = items
        valid = jnp.arange(SEQ, dtype=jnp.int32) < limit
        valid_f = valid.astype(jnp.float32)[None, None, :]
        key_f = keys.astype(jnp.float32)
        value_f = values.astype(jnp.float32)

        def one_block(block_queries):
            scores = jnp.einsum('qhd,khd->hqk', block_queries.astype(jnp.float32), key_f) * HD ** (-0.5)
            scores = jnp.where(valid[None, None, :], scores, FLOOR)
            peak = lax.optimization_barrier(jnp.max(scores, axis=-1, keepdims=True))
            probs = jnp.exp(scores - peak) * valid_f
            weight_sum = lax.optimization_barrier(jnp.sum(probs, axis=-1))
            rounded = lax.optimization_barrier(probs.astype(jnp.bfloat16))
            numer = jnp.einsum('hqk,khd->qhd', rounded.astype(jnp.float32), value_f)
            return (numer / jnp.transpose(weight_sum)[:, :, None]).astype(jnp.bfloat16)
        blocks = lax.map(one_block, queries.reshape(SEQ // block_rows, block_rows, HEADS, HD))
        return blocks.reshape(SEQ, D)
    attended = lax.map(one_video, (mixed[:, :, 0], mixed[:, :, 1], mixed[:, :, 2], lengths))
    out_proj = jnp.dot(attended.reshape(VIDEOS * SEQ, D), w_out, preferred_element_type=jnp.float32)
    out_proj = out_proj.reshape(VIDEOS, SEQ, D)
    return (hidden_states.astype(jnp.float32) + gate * out_proj).astype(jnp.bfloat16)
```

```python
import functools
import math

import jax
import jax.numpy as jnp
from jax import lax
from jax.experimental import pallas as pl
from jax.experimental.pallas import tpu as pltpu
from jax.sharding import PartitionSpec as P

HD = 128
HEADS_HERE = 3
TILE = 512
ROWS = 128
WIDTH = 1536
EPSILON = 1e-06
FLOOR = -1e30
SCORE_SCALE = HD**-0.5 * math.log2(math.e)
MESH = pl.DeviceIdType.MESH


def mod(a, n):
    return lax.rem(a + 2 * n, n)


def place():
    patch, wrow, y = lax.axis_index("patch"), lax.axis_index("wrow"), lax.axis_index("wcol")
    return patch // 4, lax.rem(patch, 4), wrow // 2, lax.rem(wrow, 2), y


def device(zh, x, zl, core, y):
    return (zh * 4 + x, zl * 2 + core, y)


def remote(src, dst, send_sem, recv_sem, target):
    return pltpu.make_async_remote_copy(
        src_ref=src,
        dst_ref=dst,
        send_sem=send_sem,
        recv_sem=recv_sem,
        device_id=target,
        device_id_type=MESH,
    )


def meet(targets):
    barrier = pltpu.get_barrier_semaphore()
    for target in targets:
        pl.semaphore_signal(barrier, inc=1, device_id=target, device_id_type=MESH)
    pl.semaphore_wait(barrier, len(targets))


def front_kernel(
    x_ref, mod_ref, w_ref, q_ref, k_ref, vt_ref, rows, weights, w_send, w_recv, y_send, y_recv, own_sem
):
    zh, x, zl, core, y = place()
    wrow = zl * 2 + core
    z = zh * 2 + zl
    up, down = mod(z + 1, 8), mod(z - 1, 8)
    other = 1 - core
    ups = [device(up // 2, x, lax.rem(up, 2), c, y) for c in (core, other)]
    downs = [device(down // 2, x, lax.rem(down, 2), c, y) for c in (core, other)]
    partner = device(zh, x, zl, other, y)
    peers = [device(zh, x, zl, core, mod(y + d, 4)) for d in (1, 2, 3)]
    meet(ups + downs + [partner] + peers)

    depth = w_ref.shape[0]
    half = depth // 2
    first = pl.multiple_of(wrow * depth, depth)
    copies = []
    for i, target in enumerate(ups):
        copies.append(
            remote(
                w_ref.at[pl.ds(half, half)],
                weights.at[pl.ds(first + half, half)],
                w_send.at[i],
                w_recv.at[i],
                target,
            )
        )
    for i, target in enumerate(downs):
        copies.append(
            remote(
                w_ref.at[pl.ds(0, half)],
                weights.at[pl.ds(first, half)],
                w_send.at[2 + i],
                w_recv.at[2 + i],
                target,
            )
        )
    copies.append(
        remote(w_ref, weights.at[pl.ds(first, depth)], w_send.at[4], w_recv.at[4], partner)
    )
    for copy in copies:
        copy.start()
    own = pltpu.make_async_copy(w_ref, weights.at[pl.ds(first, depth)], own_sem)
    own.start()

    values = x_ref[...].astype(jnp.float32)
    center = jnp.mean(values, axis=-1, keepdims=True)
    values = values - center
    spread = jnp.mean(jnp.square(values), axis=-1, keepdims=True)
    normed = values * lax.rsqrt(spread + EPSILON) * (1.0 + mod_ref[1:2]) + mod_ref[0:1]
    rows[y] = normed.astype(jnp.bfloat16)
    sends = []
    for d in (1, 3, 2):
        sends.append(remote(rows.at[y], rows.at[y], y_send.at[d], y_recv.at[d], peers[d - 1]))
    for copy in sends:
        copy.start()

    own.wait()
    for copy in copies:
        copy.wait_recv()
    for copy in sends:
        copy.wait_recv()

    flat = rows[...].reshape(4 * ROWS, WIDTH)
    cols = HEADS_HERE * HD
    part = jnp.dot(flat, weights[:, :cols], preferred_element_type=jnp.float32) * SCORE_SCALE
    for h in range(HEADS_HERE):
        q_ref[h] = part[:, h * HD : (h + 1) * HD].astype(jnp.bfloat16)
    part = jnp.dot(flat, weights[:, cols : 2 * cols], preferred_element_type=jnp.float32)
    for h in range(HEADS_HERE):
        k_ref[h] = part[:, h * HD : (h + 1) * HD].astype(jnp.bfloat16)
    part = jnp.dot(flat, weights[:, 2 * cols :], preferred_element_type=jnp.float32)
    for h in range(HEADS_HERE):
        vt_ref[h] = part[:, h * HD : (h + 1) * HD].T.astype(jnp.bfloat16)
    for copy in copies:
        copy.wait_send()
    for copy in sends:
        copy.wait_send()


def front(states, modulation, weights):
    vmem = pl.BlockSpec(memory_space=pltpu.VMEM)
    return pl.pallas_call(
        front_kernel,
        name="front",
        out_shape=(
            jax.ShapeDtypeStruct((HEADS_HERE, TILE, HD), jnp.bfloat16),
            jax.ShapeDtypeStruct((HEADS_HERE, TILE, HD), jnp.bfloat16),
            jax.ShapeDtypeStruct((HEADS_HERE, HD, TILE), jnp.bfloat16),
        ),
        in_specs=[vmem] * 3,
        out_specs=[vmem] * 3,
        scratch_shapes=[
            pltpu.VMEM((4, ROWS, WIDTH), jnp.bfloat16),
            pltpu.VMEM((WIDTH, 3 * HEADS_HERE * HD), jnp.bfloat16),
            pltpu.SemaphoreType.DMA((5,)),
            pltpu.SemaphoreType.DMA((5,)),
            pltpu.SemaphoreType.DMA((4,)),
            pltpu.SemaphoreType.DMA((4,)),
            pltpu.SemaphoreType.DMA,
        ],
        compiler_params=pltpu.CompilerParams(
            collective_id=0, has_side_effects=True, vmem_limit_bytes=40 << 20
        ),
    )(states, modulation, weights)


ORDER = (
    (0, 0), (0, 1), (0, 3), (1, 0), (0, 2), (3, 0), (1, 1), (1, 3),
    (2, 0), (3, 1), (3, 3), (1, 2), (2, 1), (2, 3), (3, 2), (2, 2),
)


def attend_kernel(
    len_ref, q_in, k_in, vt_in, out_ref,
    q_buf, k_buf, vt_buf, peak_ref, sum_ref, numer_ref, done_buf, att_buf,
    z_send, z_recv, x_send, x_recv, o_send, o_recv, own_sem,
):
    zh, x, zl, core, y = place()
    video = zl * 2 + core
    limit = len_ref[0]

    def head_of(row):
        return mod(row - video - 1, 4)

    head = head_of(zh)
    active = head < HEADS_HERE
    right, left = device(zh, mod(x + 1, 4), zl, core, y), device(zh, mod(x - 1, 4), zl, core, y)
    row_devices = {}
    for dz in range(4):
        for dy in range(4):
            row_devices[dz, dy] = device(mod(zh + dz, 4), x, zl, core, mod(y + dy, 4))
    meet([right, left] + [row_devices[key] for key in row_devices if key != (0, 0)])

    def z_copies(d):
        there = head_of(mod(zh + d, 4))
        there = jnp.minimum(there, HEADS_HERE - 1)
        block = zh * 4 + x
        target = row_devices[d, 0]
        return (
            remote(q_in.at[there], q_buf.at[zh], z_send.at[0, d], z_recv.at[0, d], target),
            remote(k_in.at[there], k_buf.at[block], z_send.at[1, d], z_recv.at[1, d], target),
            remote(vt_in.at[there], vt_buf.at[block], z_send.at[2, d], z_recv.at[2, d], target),
        )

    def sends_to(d):
        return head_of(mod(zh + d, 4)) < HEADS_HERE

    for which in range(3):
        for d in (1, 3, 2):
            @pl.when(sends_to(d))
            def _():
                z_copies(d)[which].start()

    def x_copies(d):
        source = mod(zh - d, 4)
        mine = source * 4 + x
        from_left = source * 4 + mod(x - 1, 4)
        from_right = source * 4 + mod(x + 1, 4)

        def one(buf, block, i, target):
            return remote(buf.at[block], buf.at[block], x_send.at[d, i], x_recv.at[d, i], target)

        return (
            one(k_buf, mine, 0, right),
            one(vt_buf, mine, 1, right),
            one(k_buf, mine, 2, left),
            one(vt_buf, mine, 3, left),
            one(k_buf, from_left, 4, right),
            one(vt_buf, from_right, 5, left),
        )

    def spread(d):
        for copy in x_copies(d)[:4]:
            copy.start()

    def wait_z(d):
        z_copies(d)[1].wait_recv()
        z_copies(d)[2].wait_recv()

    def pass_on(d):
        copies = x_copies(d)
        for copy in copies[:4]:
            copy.wait_recv()
        copies[4].start()
        copies[5].start()

    def wait_far(d):
        copies = x_copies(d)
        copies[4].wait_recv()
        copies[5].wait_recv()

    def out_copy(dz, dy):
        tile = mod(zh + dz, 4)
        part = mod(y + dy, 4)
        first = pl.multiple_of(tile * TILE + part * ROWS, ROWS)
        column = pl.multiple_of((y * HEADS_HERE + jnp.minimum(head, HEADS_HERE - 1)) * HD, HD)
        i = dz * 4 + dy
        src = done_buf.at[pl.ds(first, ROWS)]
        dst = att_buf.at[:, pl.ds(column, HD)]
        if i == 0:
            return pltpu.make_async_copy(src, dst, o_send.at[0])
        return remote(src, dst, o_send.at[i], o_recv.at[i], row_devices[dz, dy])

    @pl.when(active)
    def _():
        block = zh * 4 + x
        mine = jnp.minimum(head, HEADS_HERE - 1)
        own = (
            pltpu.make_async_copy(q_in.at[mine], q_buf.at[zh], own_sem.at[0]),
            pltpu.make_async_copy(k_in.at[mine], k_buf.at[block], own_sem.at[1]),
            pltpu.make_async_copy(vt_in.at[mine], vt_buf.at[block], own_sem.at[2]),
        )
        for copy in own:
            copy.start()
        for copy in own:
            copy.wait()
        spread(0)
        peak_ref[...] = jnp.full_like(peak_ref, FLOOR)
        sum_ref[...] = jnp.zeros_like(sum_ref)
        numer_ref[...] = jnp.zeros_like(numer_ref)
        for d in (1, 3, 2):
            z_copies(d)[0].wait_recv()

        def step(i, carry):
            before = {
                1: lambda: pass_on(0),
                3: lambda: (wait_z(1), spread(1)),
                4: lambda: wait_far(0),
                5: lambda: (wait_z(3), spread(3)),
                6: lambda: pass_on(1),
                8: lambda: (wait_z(2), spread(2)),
                9: lambda: pass_on(3),
                11: lambda: wait_far(1),
                12: lambda: pass_on(2),
                14: lambda: wait_far(3),
                15: lambda: wait_far(2),
            }
            for at, act in before.items():
                @pl.when(i == at)
                def _():
                    act()
            back_z, back_x = 0, 0
            for at, (dz, dx) in enumerate(ORDER):
                back_z = jnp.where(i == at, dz, back_z)
                back_x = jnp.where(i == at, dx, back_x)
            block = mod(zh - back_z, 4) * 4 + mod(x - back_x, 4)
            queries = q_buf[...].reshape(4 * TILE, HD)
            scores = lax.dot_general(
                k_buf[block], queries, (((1,), (1,)), ((), ())), preferred_element_type=jnp.float32
            )
            position = block * TILE + lax.broadcasted_iota(jnp.int32, (TILE, 1), 0)
            scores = scores + jnp.where(position < limit, 0.0, FLOOR)
            peak = peak_ref[...]
            new_peak = jnp.maximum(peak, jnp.max(scores, axis=0, keepdims=True))
            factor = jnp.exp2(peak - new_peak)
            probs = jnp.exp2(scores - new_peak).astype(jnp.bfloat16)
            with_ones = jnp.concatenate([vt_buf[block], jnp.ones((16, TILE), jnp.bfloat16)], 0)
            mixed = jnp.dot(with_ones, probs, preferred_element_type=jnp.float32)
            peak_ref[...] = new_peak
            sum_ref[...] = sum_ref[...] * factor + mixed[HD : HD + 1]
            numer_ref[...] = numer_ref[...] * factor + mixed[:HD]
            return carry

        lax.fori_loop(0, 16, step, 0)
        attended = numer_ref[...] / sum_ref[...]
        done_buf[...] = attended.T.astype(jnp.bfloat16)
        for dz in range(4):
            for dy in range(4):
                out_copy(dz, dy).start()
        for d in range(4):
            for copy in x_copies(d):
                copy.wait_send()
        out_copy(0, 0).wait()
        for dz in range(4):
            for dy in range(4):
                if dz + dy > 0:
                    out_copy(dz, dy).wait_send()

    for d in (1, 3, 2):
        @pl.when(sends_to(d))
        def _():
            for copy in z_copies(d):
                copy.wait_send()

    for dz in range(4):
        @pl.when(head_of(mod(zh - dz, 4)) < HEADS_HERE)
        def _():
            for dy in range(4):
                if dz + dy > 0:
                    out_copy(dz, dy).wait_recv()
    out_ref[...] = att_buf[...]


def attend(lengths, q, k, vt):
    vmem = pl.BlockSpec(memory_space=pltpu.VMEM)
    return pl.pallas_call(
        attend_kernel,
        name="attend",
        out_shape=jax.ShapeDtypeStruct((ROWS, WIDTH), jnp.bfloat16),
        in_specs=[pl.BlockSpec(memory_space=pltpu.SMEM)] + [vmem] * 3,
        out_specs=vmem,
        scratch_shapes=[
            pltpu.VMEM((4, TILE, HD), jnp.bfloat16),
            pltpu.VMEM((16, TILE, HD), jnp.bfloat16),
            pltpu.VMEM((16, HD, TILE), jnp.bfloat16),
            pltpu.VMEM((1, 4 * TILE), jnp.float32),
            pltpu.VMEM((1, 4 * TILE), jnp.float32),
            pltpu.VMEM((HD, 4 * TILE), jnp.float32),
            pltpu.VMEM((4 * TILE, HD), jnp.bfloat16),
            pltpu.VMEM((ROWS, WIDTH), jnp.bfloat16),
            pltpu.SemaphoreType.DMA((3, 4)),
            pltpu.SemaphoreType.DMA((3, 4)),
            pltpu.SemaphoreType.DMA((4, 6)),
            pltpu.SemaphoreType.DMA((4, 6)),
            pltpu.SemaphoreType.DMA((16,)),
            pltpu.SemaphoreType.DMA((16,)),
            pltpu.SemaphoreType.DMA((3,)),
        ],
        compiler_params=pltpu.CompilerParams(
            collective_id=1, has_side_effects=True, vmem_limit_bytes=48 << 20
        ),
    )(lengths, q, k, vt)


def body(hidden_states, modulation, w_qkv, w_out, lengths):
    states = hidden_states[0]
    w_full = lax.all_gather(w_out, "wrow", axis=1, tiled=True)
    w_full = lax.all_gather(w_full, "wcol", axis=0, tiled=True)
    q, k, vt = front(states, modulation[0], w_qkv.reshape(w_qkv.shape[0], -1))
    attended = attend(lengths, q, k, vt)
    out_proj = jnp.dot(attended, w_full, preferred_element_type=jnp.float32)
    gate = modulation[0, 2][None]
    return (states.astype(jnp.float32) + gate * out_proj).astype(jnp.bfloat16)[None]


def solution(mesh):
    placed = (
        P("wrow", ("patch", "wcol"), None),
        P("wrow", None, None),
        P("wrow", None, "wcol"),
        P("wcol", "wrow"),
        P("wrow"),
    )
    return jax.shard_map(
        body,
        mesh=mesh,
        in_specs=placed,
        out_specs=P("wrow", ("patch", "wcol"), None),
        check_vma=False,
    )
```

```python
import math

import jax
import jax.numpy as jnp
from jax import lax
from jax.experimental import pallas as pl
from jax.experimental.pallas import tpu as pltpu
from jax.sharding import PartitionSpec as P

HD = 128
HEADS_HERE = 3
TILE = 512
ROWS = 128
WIDTH = 1536
PART = 384
HALF = PART // 2
EPSILON = 1e-06
FLOOR = -1e30
SCORE_SCALE = HD**-0.5 * math.log2(math.e)
MESH = pl.DeviceIdType.MESH

ORDER = (
    (0, 0), (0, 1), (0, 3), (1, 0), (0, 2), (3, 0), (1, 1), (1, 3),
    (2, 0), (3, 1), (3, 3), (1, 2), (2, 1), (2, 3), (3, 2), (2, 2),
)


def mod(a, n):
    return lax.rem(a + 2 * n, n)


def device(zh, x, zl, core, y):
    return (zh * 4 + x, zl * 2 + core, y)


def remote(src, dst, send_sem, recv_sem, target):
    return pltpu.make_async_remote_copy(
        src_ref=src,
        dst_ref=dst,
        send_sem=send_sem,
        recv_sem=recv_sem,
        device_id=target,
        device_id_type=MESH,
    )


def kernel(
    len_ref, x_ref, mod_ref, w_ref, wo_ref, out_ref,
    rows, weights, wo_buf, q_in, k_in, vt_in,
    q_buf, k_buf, vt_buf, peak_ref, sum_ref, numer_ref, done_buf, att_buf,
    w_send, w_recv, a_send, a_recv, b_send, b_recv, r_send, r_recv, y_send, y_recv,
    z_send, z_recv, x_send, x_recv, o_send, o_recv, own_sem,
):
    patch, video, y = lax.axis_index("patch"), lax.axis_index("wrow"), lax.axis_index("wcol")
    zh, x = patch // 4, lax.rem(patch, 4)
    zl, core = video // 2, lax.rem(video, 2)
    z = zh * 2 + zl
    limit = len_ref[0]

    def at(dzh=0, dx=0, dy=0):
        return device(mod(zh + dzh, 4), mod(x + dx, 4), zl, core, mod(y + dy, 4))

    up_z, down_z = mod(z + 1, 8), mod(z - 1, 8)
    up = device(up_z // 2, x, lax.rem(up_z, 2), core, y)
    down = device(down_z // 2, x, lax.rem(down_z, 2), core, y)
    partner = device(zh, x, zl, 1 - core, y)
    right, left = at(dx=1), at(dx=-1)

    barrier = pltpu.get_barrier_semaphore()
    targets = [up, down, partner, right, left]
    targets += [at(dzh=dz, dy=dy) for dz in range(4) for dy in range(4) if dz + dy > 0]
    for target in targets:
        pl.semaphore_signal(barrier, inc=1, device_id=target, device_id_type=MESH)
    pl.semaphore_wait(barrier, len(targets))

    mine_first = pl.multiple_of(video * PART, PART)
    theirs_first = pl.multiple_of(((1 - zl) * 2 + core) * PART, PART)

    def w_copy(i):
        if i == 0:
            src, first, count, target = w_ref.at[:, pl.ds(HALF, HALF)], mine_first + HALF, HALF, up
        elif i == 1:
            src, first, count, target = w_ref.at[:, pl.ds(0, HALF)], mine_first, HALF, down
        elif i == 2:
            src, first, count, target = w_ref, mine_first, PART, partner
        else:
            first, count, target = theirs_first + (HALF if i == 3 else 0), HALF, partner
            src = weights.at[:, pl.ds(first, count)]
        return remote(src, weights.at[:, pl.ds(first, count)], w_send.at[i], w_recv.at[i], target)

    wo_rows = pl.multiple_of(y * PART, PART)

    def a_copy(i):
        first = wo_rows + (HALF if i in (0, 3) else 0)
        count = PART if i == 2 else HALF
        column = mine_first if i < 3 else theirs_first
        target = (up, down, partner, partner, partner)[i]
        src = wo_buf.at[pl.ds(first, count), pl.ds(column, PART)]
        return remote(src, src, a_send.at[i], a_recv.at[i], target)

    def b_copy(d):
        part = wo_buf.at[pl.ds(wo_rows + core * HALF, HALF)]
        return remote(part, part, b_send.at[d], b_recv.at[d], at(dy=d))

    def r_copy(d):
        part = wo_buf.at[pl.ds(mod(y - d, 4) * PART + core * HALF, HALF)]
        return remote(part, part, r_send.at[d], r_recv.at[d], partner)

    def own_w():
        return pltpu.make_async_copy(w_ref, weights.at[:, pl.ds(mine_first, PART)], own_sem.at[3])

    def own_wo():
        return pltpu.make_async_copy(
            wo_ref, wo_buf.at[pl.ds(wo_rows, PART), pl.ds(mine_first, PART)], own_sem.at[4]
        )

    def y_copy(d):
        return remote(rows.at[y], rows.at[y], y_send.at[d], y_recv.at[d], at(dy=d))

    for i in (0, 1, 2):
        w_copy(i).start()
    own_w().start()
    own_wo().start()

    values = x_ref[...].astype(jnp.float32)
    center = jnp.mean(values, axis=-1, keepdims=True)
    values = values - center
    spread = jnp.mean(jnp.square(values), axis=-1, keepdims=True)
    normed = values * lax.rsqrt(spread + EPSILON) * (1.0 + mod_ref[1]) + mod_ref[0]
    rows[y] = normed.astype(jnp.bfloat16)
    for d in (1, 3, 2):
        y_copy(d).start()

    own_wo().wait()
    for i in (0, 1):
        w_copy(i).wait_recv()
        w_copy(3 + i).start()
    for i in (0, 1, 2):
        a_copy(i).start()
    own_w().wait()
    for i in (2, 3, 4):
        w_copy(i).wait_recv()
    for d in (1, 3, 2):
        y_copy(d).wait_recv()

    def head_of(row):
        return mod(row - video - 1, 4)

    head = head_of(zh)
    active = head < HEADS_HERE
    head = jnp.minimum(head, HEADS_HERE - 1)
    own_block = zh * 4 + x
    z_refs = ((q_in, q_buf, zh), (k_in, k_buf, own_block), (vt_in, vt_buf, own_block))

    def z_copy(which, d):
        source, dest, index = z_refs[which]
        there = jnp.minimum(head_of(mod(zh + d, 4)), HEADS_HERE - 1)
        return remote(
            source.at[there], dest.at[index], z_send.at[which, d], z_recv.at[which, d], at(dzh=d)
        )

    def sends_to(d):
        return head_of(mod(zh + d, 4)) < HEADS_HERE

    def own_copy(which):
        source, dest, index = z_refs[which]
        return pltpu.make_async_copy(source.at[head], dest.at[index], own_sem.at[which])

    def hand_out(which):
        @pl.when(active)
        def _():
            own_copy(which).start()

        for d in (1, 3, 2):
            @pl.when(sends_to(d))
            def _():
                z_copy(which, d).start()

    flat = rows[...].reshape(4 * ROWS, WIDTH)
    for which in range(3):
        part = jnp.dot(flat, weights[which], preferred_element_type=jnp.float32)
        if which == 0:
            part = part * SCORE_SCALE
        for h in range(HEADS_HERE):
            one = part[:, h * HD : (h + 1) * HD]
            if which == 2:
                vt_in[h] = one.T.astype(jnp.bfloat16)
            else:
                z_refs[which][0][h] = one.astype(jnp.bfloat16)
        hand_out(which)

    for i in (0, 1):
        a_copy(i).wait_recv()
        a_copy(3 + i).start()

    def x_copy(d, i):
        source = mod(zh - d, 4)
        column = (x, x, x, x, mod(x - 1, 4), mod(x + 1, 4))[i]
        buf = (k_buf, vt_buf, k_buf, vt_buf, k_buf, vt_buf)[i]
        target = (right, right, left, left, right, left)[i]
        block = source * 4 + column
        return remote(buf.at[block], buf.at[block], x_send.at[d, i], x_recv.at[d, i], target)

    def spread_out(d):
        for i in range(4):
            x_copy(d, i).start()

    def wait_z(d):
        z_copy(1, d).wait_recv()
        z_copy(2, d).wait_recv()

    def pass_on(d):
        for i in range(4):
            x_copy(d, i).wait_recv()
        x_copy(d, 4).start()
        x_copy(d, 5).start()

    def wait_far(d):
        x_copy(d, 4).wait_recv()
        x_copy(d, 5).wait_recv()

    def out_copy(dz, dy):
        first = pl.multiple_of(mod(zh + dz, 4) * TILE + mod(y + dy, 4) * ROWS, ROWS)
        column = pl.multiple_of((y * HEADS_HERE + head) * HD, HD)
        i = dz * 4 + dy
        src = done_buf.at[pl.ds(first, ROWS)]
        dst = att_buf.at[:, pl.ds(column, HD)]
        if i == 0:
            return pltpu.make_async_copy(src, dst, o_send.at[0])
        return remote(src, dst, o_send.at[i], o_recv.at[i], at(dzh=dz, dy=dy))

    def start_b():
        for i in (2, 3, 4):
            a_copy(i).wait_recv()
        for d in (1, 3, 2):
            b_copy(d).start()

    def relay_b():
        for d in (1, 3, 2):
            b_copy(d).wait_recv()
            r_copy(d).start()

    @pl.when(active)
    def _():
        for which in range(3):
            own_copy(which).wait()
        spread_out(0)
        peak_ref[...] = jnp.full_like(peak_ref, FLOOR)
        sum_ref[...] = jnp.zeros_like(sum_ref)
        numer_ref[...] = jnp.zeros_like(numer_ref)
        for d in (1, 3, 2):
            z_copy(0, d).wait_recv()

    start_b()

    @pl.when(active)
    def _():
        def step(i, carry):
            before = {
                1: lambda: pass_on(0),
                3: lambda: (wait_z(1), spread_out(1)),
                4: lambda: wait_far(0),
                5: lambda: (wait_z(3), spread_out(3)),
                6: lambda: pass_on(1),
                8: lambda: (wait_z(2), spread_out(2)),
                9: lambda: pass_on(3),
                11: lambda: wait_far(1),
                12: lambda: pass_on(2),
                14: lambda: wait_far(3),
                15: lambda: wait_far(2),
            }
            for when, act in before.items():
                @pl.when(i == when)
                def _():
                    act()
            back_z, back_x = 0, 0
            for when, (dz, dx) in enumerate(ORDER):
                back_z = jnp.where(i == when, dz, back_z)
                back_x = jnp.where(i == when, dx, back_x)
            block = mod(zh - back_z, 4) * 4 + mod(x - back_x, 4)
            queries = q_buf[...].reshape(4 * TILE, HD)
            scores = lax.dot_general(
                k_buf[block], queries, (((1,), (1,)), ((), ())), preferred_element_type=jnp.float32
            )
            position = block * TILE + lax.broadcasted_iota(jnp.int32, (TILE, 1), 0)
            scores = scores + jnp.where(position < limit, 0.0, FLOOR)
            peak = peak_ref[...]
            new_peak = jnp.maximum(peak, jnp.max(scores, axis=0, keepdims=True))
            factor = jnp.exp2(peak - new_peak)
            probs = jnp.exp2(scores - new_peak).astype(jnp.bfloat16)
            with_ones = jnp.concatenate([vt_buf[block], jnp.ones((16, TILE), jnp.bfloat16)], 0)
            mixed = jnp.dot(with_ones, probs, preferred_element_type=jnp.float32)
            peak_ref[...] = new_peak
            sum_ref[...] = sum_ref[...] * factor + mixed[HD : HD + 1]
            numer_ref[...] = numer_ref[...] * factor + mixed[:HD]
            return carry

        lax.fori_loop(0, 16, step, 0)
        attended = numer_ref[...] / sum_ref[...]
        done_buf[...] = attended.T.astype(jnp.bfloat16)
        for dz in range(4):
            for dy in range(4):
                out_copy(dz, dy).start()

    relay_b()
    for d in (1, 3, 2):
        r_copy(d).wait_recv()

    @pl.when(active)
    def _():
        out_copy(0, 0).wait()

    for dz in range(4):
        @pl.when(head_of(mod(zh - dz, 4)) < HEADS_HERE)
        def _():
            for dy in range(4):
                if dz + dy > 0:
                    out_copy(dz, dy).wait_recv()

    out_proj = jnp.dot(att_buf[...], wo_buf[...], preferred_element_type=jnp.float32)
    out_ref[...] = (x_ref[...].astype(jnp.float32) + mod_ref[2] * out_proj).astype(jnp.bfloat16)

    for i in range(5):
        w_copy(i).wait_send()
        a_copy(i).wait_send()
    for d in (1, 3, 2):
        y_copy(d).wait_send()
        b_copy(d).wait_send()
        r_copy(d).wait_send()

        @pl.when(sends_to(d))
        def _():
            for which in range(3):
                z_copy(which, d).wait_send()

    @pl.when(active)
    def _():
        for d in range(4):
            for i in range(6):
                x_copy(d, i).wait_send()
        for dz in range(4):
            for dy in range(4):
                if dz + dy > 0:
                    out_copy(dz, dy).wait_send()


def body(hidden_states, modulation, w_qkv, w_out, lengths):
    vmem = pl.BlockSpec(memory_space=pltpu.VMEM)
    dma = pltpu.SemaphoreType.DMA
    bf16 = jnp.bfloat16
    updated = pl.pallas_call(
        kernel,
        name="block",
        out_shape=jax.ShapeDtypeStruct((ROWS, WIDTH), bf16),
        in_specs=[pl.BlockSpec(memory_space=pltpu.SMEM)] + [vmem] * 4,
        out_specs=vmem,
        scratch_shapes=[
            pltpu.VMEM((4, ROWS, WIDTH), bf16),
            pltpu.VMEM((3, WIDTH, PART), bf16),
            pltpu.VMEM((WIDTH, WIDTH), bf16),
            pltpu.VMEM((HEADS_HERE, TILE, HD), bf16),
            pltpu.VMEM((HEADS_HERE, TILE, HD), bf16),
            pltpu.VMEM((HEADS_HERE, HD, TILE), bf16),
            pltpu.VMEM((4, TILE, HD), bf16),
            pltpu.VMEM((16, TILE, HD), bf16),
            pltpu.VMEM((16, HD, TILE), bf16),
            pltpu.VMEM((1, 4 * TILE), jnp.float32),
            pltpu.VMEM((1, 4 * TILE), jnp.float32),
            pltpu.VMEM((HD, 4 * TILE), jnp.float32),
            pltpu.VMEM((4 * TILE, HD), bf16),
            pltpu.VMEM((ROWS, WIDTH), bf16),
            dma((5,)), dma((5,)), dma((5,)), dma((5,)),
            dma((4,)), dma((4,)), dma((4,)), dma((4,)), dma((4,)), dma((4,)),
            dma((3, 4)), dma((3, 4)), dma((4, 6)), dma((4, 6)), dma((16,)), dma((16,)), dma((5,)),
        ],
        compiler_params=pltpu.CompilerParams(
            collective_id=0, has_side_effects=True, vmem_limit_bytes=56 << 20
        ),
    )(
        lengths,
        hidden_states[0],
        jnp.transpose(modulation, (1, 0, 2)),
        jnp.transpose(w_qkv, (1, 0, 2)),
        w_out,
    )
    return updated[None]


def solution(mesh):
    placed = (
        P("wrow", ("patch", "wcol"), None),
        P("wrow", None, None),
        P("wrow", None, "wcol"),
        P("wcol", "wrow"),
        P("wrow"),
    )
    return jax.shard_map(
        body,
        mesh=mesh,
        in_specs=placed,
        out_specs=P("wrow", ("patch", "wcol"), None),
        check_vma=False,
    )
```

```python
import math

import jax
import jax.numpy as jnp
from jax import lax
from jax.experimental import pallas as pl
from jax.experimental.pallas import tpu as pltpu
from jax.sharding import PartitionSpec as P

HD = 128
HEADS_HERE = 3
TILE = 512
ROWS = 128
WIDTH = 1536
PART = 384
HALF = PART // 2
EPSILON = 1e-06
FLOOR = -1e30
SCORE_SCALE = HD**-0.5 * math.log2(math.e)
MESH = pl.DeviceIdType.MESH

SLOTS = (0, 1, 3, 2)
HALF_ROWS = ROWS // 2
SPAN = (slice(0, 3 * ROWS), slice(3 * ROWS, 4 * ROWS))

ORDER = (
    (0, 0), (0, 1), (0, 3), (1, 0), (0, 2), (3, 0), (1, 1), (1, 3),
    (2, 0), (3, 1), (3, 3), (1, 2), (2, 1), (2, 3), (3, 2), (2, 2),
)


def mod(a, n):
    return lax.rem(a + 2 * n, n)


def device(zh, x, zl, core, y):
    return (zh * 4 + x, zl * 2 + core, y)


def remote(src, dst, send_sem, recv_sem, target):
    return pltpu.make_async_remote_copy(
        src_ref=src,
        dst_ref=dst,
        send_sem=send_sem,
        recv_sem=recv_sem,
        device_id=target,
        device_id_type=MESH,
    )


def kernel(
    len_ref, x_ref, mod_ref, w_ref, wo_ref, out_ref,
    rows, weights, wo_buf, q_in, k_in, vt_in,
    rq_buf, rk_buf, rv_buf, q_buf, k_buf, vt_buf, peak_ref, sum_ref, numer_ref, done_buf, att_buf,
    w_send, w_recv, a_send, a_recv, b_send, b_recv, r_send, r_recv, y_send, y_recv,
    h_send, h_recv, z_send, z_recv, x_send, x_recv, o_send, o_recv, own_sem,
):
    patch, video, y = lax.axis_index("patch"), lax.axis_index("wrow"), lax.axis_index("wcol")
    zh, x = patch // 4, lax.rem(patch, 4)
    zl, core = video // 2, lax.rem(video, 2)
    z = zh * 2 + zl
    limit = len_ref[0]

    def at(dzh=0, dx=0, dy=0):
        return device(mod(zh + dzh, 4), mod(x + dx, 4), zl, core, mod(y + dy, 4))

    up_z, down_z = mod(z + 1, 8), mod(z - 1, 8)
    up = device(up_z // 2, x, lax.rem(up_z, 2), core, y)
    down = device(down_z // 2, x, lax.rem(down_z, 2), core, y)
    partner = device(zh, x, zl, 1 - core, y)
    right, left = at(dx=1), at(dx=-1)

    barrier = pltpu.get_barrier_semaphore()
    targets = [up, down, partner, right, left]
    targets += [at(dzh=dz, dy=dy) for dz in range(4) for dy in range(4) if dz + dy > 0]
    for target in targets:
        pl.semaphore_signal(barrier, inc=1, device_id=target, device_id_type=MESH)
    pl.semaphore_wait(barrier, len(targets))

    mine_first = pl.multiple_of(video * PART, PART)
    theirs_first = pl.multiple_of(((1 - zl) * 2 + core) * PART, PART)

    def w_copy(i):
        if i == 0:
            src, first, count, target = w_ref.at[:, pl.ds(HALF, HALF)], mine_first + HALF, HALF, up
        elif i == 1:
            src, first, count, target = w_ref.at[:, pl.ds(0, HALF)], mine_first, HALF, down
        elif i == 2:
            src, first, count, target = w_ref, mine_first, PART, partner
        else:
            first, count, target = theirs_first + (HALF if i == 3 else 0), HALF, partner
            src = weights.at[:, pl.ds(first, count)]
        return remote(src, weights.at[:, pl.ds(first, count)], w_send.at[i], w_recv.at[i], target)

    wo_rows = pl.multiple_of(y * PART, PART)

    def a_copy(i):
        first = wo_rows + (HALF if i in (0, 3) else 0)
        count = PART if i == 2 else HALF
        column = mine_first if i < 3 else theirs_first
        target = (up, down, partner, partner, partner)[i]
        src = wo_buf.at[pl.ds(first, count), pl.ds(column, PART)]
        return remote(src, src, a_send.at[i], a_recv.at[i], target)

    def b_copy(d):
        part = wo_buf.at[pl.ds(wo_rows + core * HALF, HALF)]
        return remote(part, part, b_send.at[d], b_recv.at[d], at(dy=d))

    def r_copy(d):
        part = wo_buf.at[pl.ds(mod(y - d, 4) * PART + core * HALF, HALF)]
        return remote(part, part, r_send.at[d], r_recv.at[d], partner)

    def own_w():
        return pltpu.make_async_copy(w_ref, weights.at[:, pl.ds(mine_first, PART)], own_sem.at[6])

    def own_wo():
        return pltpu.make_async_copy(
            wo_ref, wo_buf.at[pl.ds(wo_rows, PART), pl.ds(mine_first, PART)], own_sem.at[7]
        )

    def y_copy(i):
        src = rows.at[0] if i < 2 else rows.at[i - 1, pl.ds((i - 2) * HALF_ROWS, HALF_ROWS)]
        dst = rows.at[1 + i] if i < 2 else rows.at[3, pl.ds((i - 2) * HALF_ROWS, HALF_ROWS)]
        target = at(dy=1) if i in (0, 2) else at(dy=-1)
        return remote(src, dst, y_send.at[i], y_recv.at[i], target)

    for i in (0, 1, 2):
        w_copy(i).start()
    own_w().start()
    own_wo().start()

    values = x_ref[...].astype(jnp.float32)
    center = jnp.mean(values, axis=-1, keepdims=True)
    values = values - center
    spread = jnp.mean(jnp.square(values), axis=-1, keepdims=True)
    normed = values * lax.rsqrt(spread + EPSILON) * (1.0 + mod_ref[1]) + mod_ref[0]
    rows[0] = normed.astype(jnp.bfloat16)
    for i in (0, 1):
        y_copy(i).start()

    for i in (0, 1):
        w_copy(i).wait_recv()
        w_copy(3 + i).start()
    for i in (0, 1):
        y_copy(i).wait_recv()
        y_copy(2 + i).start()
    own_w().wait()
    for i in (2, 3, 4):
        w_copy(i).wait_recv()

    idle = lax.rem(video, 2) * 2 + video // 2

    def head_of(row):
        return mod(row - idle - 1, 4)

    head = head_of(zh)
    active = head < HEADS_HERE
    head = jnp.minimum(head, HEADS_HERE - 1)
    own_block = zh * 4 + x

    def cut(ref, which, g):
        return ref.at[:, SPAN[g]] if which == 2 else ref.at[SPAN[g]]

    z_in, z_buf = (q_in, k_in, vt_in), (q_buf, k_buf, vt_buf)
    turn = 1 - 2 * core

    def takes(d):
        return head_of(mod(zh + d, 4)) < HEADS_HERE

    def tile_index(which, row):
        return row if which == 0 else row * 4 + x

    def z_copy(which, g, d):
        there = jnp.minimum(head_of(mod(zh + d, 4)), HEADS_HERE - 1)
        return remote(
            cut(z_in[which].at[there], which, g),
            cut(z_buf[which].at[tile_index(which, zh)], which, g),
            z_send.at[which * 2 + g, d],
            z_recv.at[which * 2 + g, d],
            at(dzh=d),
        )

    def way(which):
        return -turn if which == 2 else turn

    def first_hop(which, g):
        there = jnp.minimum(head_of(mod(zh + 2, 4)), HEADS_HERE - 1)
        return remote(
            cut(z_in[which].at[there], which, g),
            cut((rq_buf, rk_buf, rv_buf)[which], which, g),
            h_send.at[which * 2 + g],
            h_recv.at[which * 2 + g],
            at(dzh=way(which)),
        )

    def second_hop(which, g):
        source = mod(zh - way(which), 4)
        return remote(
            cut((rq_buf, rk_buf, rv_buf)[which], which, g),
            cut(z_buf[which].at[tile_index(which, source)], which, g),
            z_send.at[which * 2 + g, 2],
            z_recv.at[which * 2 + g, 2],
            at(dzh=way(which)),
        )

    def own_copy(which, g):
        return pltpu.make_async_copy(
            cut(z_in[which].at[head], which, g),
            cut(z_buf[which].at[tile_index(which, zh)], which, g),
            own_sem.at[which * 2 + g],
        )

    def x_copy(d, g, i):
        source = mod(zh - d, 4)
        column = (x, x, x, x, mod(x - 1, 4), mod(x + 1, 4))[i]
        which = 1 + i % 2
        target = (right, right, left, left, right, left)[i]
        block = source * 4 + column
        dst = cut(z_buf[which].at[block], which, g)
        src = cut(z_in[which].at[head], which, g) if d == 0 and i < 4 else dst
        return remote(src, dst, x_send.at[d * 2 + g, i], x_recv.at[d * 2 + g, i], target)

    def spread_out(d, g):
        for i in range(4):
            x_copy(d, g, i).start()

    def project(g, first, count):
        flat = rows[pl.ds(first, count)].reshape(count * ROWS, WIDTH)
        for which in range(3):
            part = jnp.dot(flat, weights[which], preferred_element_type=jnp.float32)
            if which == 0:
                part = part * SCORE_SCALE
            for h in range(HEADS_HERE):
                one = part[:, h * HD : (h + 1) * HD]
                if which == 2:
                    vt_in[h, :, SPAN[g]] = one.T.astype(jnp.bfloat16)
                else:
                    z_in[which][h, SPAN[g]] = one.astype(jnp.bfloat16)

            @pl.when(takes(2))
            def _():
                first_hop(which, g).start()

            for d in (1, 3):
                @pl.when(takes(d))
                def _():
                    z_copy(which, g, d).start()

            @pl.when(active)
            def _():
                own_copy(which, g).start()

        @pl.when(active)
        def _():
            spread_out(0, g)

    def relay(g):
        for which in range(3):
            @pl.when(head_of(mod(zh + way(which), 4)) < HEADS_HERE)
            def _():
                first_hop(which, g).wait_recv()
                second_hop(which, g).start()

    def wait_z(d, g):
        z_copy(1, g, d).wait_recv()
        z_copy(2, g, d).wait_recv()

    project(0, 0, 3)
    for i in (2, 3):
        y_copy(i).wait_recv()
    project(1, 3, 1)
    own_wo().wait()
    for i in (0, 1, 2):
        a_copy(i).start()
    relay(0)

    @pl.when(active)
    def _():
        for d in (1, 3):
            wait_z(d, 0)
            spread_out(d, 0)

    relay(1)

    @pl.when(active)
    def _():
        for d in (1, 3):
            wait_z(d, 1)
            spread_out(d, 1)

    for i in (0, 1):
        a_copy(i).wait_recv()
        a_copy(3 + i).start()

    def pass_on(d):
        for g in range(2):
            for i in range(4):
                x_copy(d, g, i).wait_recv()
            x_copy(d, g, 4).start()
            x_copy(d, g, 5).start()

    def wait_far(d):
        for g in range(2):
            x_copy(d, g, 4).wait_recv()
            x_copy(d, g, 5).wait_recv()

    def last_row():
        for g in range(2):
            wait_z(2, g)
            spread_out(2, g)

    def out_copy(dz, slot):
        first = pl.multiple_of(mod(zh + dz, 4) * TILE + slot * ROWS, ROWS)
        column = pl.multiple_of((y * HEADS_HERE + head) * HD, HD)
        i = dz * 4 + slot
        src = done_buf.at[pl.ds(first, ROWS)]
        dst = att_buf.at[:, pl.ds(column, HD)]
        if i == 0:
            return pltpu.make_async_copy(src, dst, o_send.at[0])
        return remote(src, dst, o_send.at[i], o_recv.at[i], at(dzh=dz, dy=-SLOTS[slot]))

    def start_b():
        for i in (2, 3, 4):
            a_copy(i).wait_recv()
        for d in (1, 3, 2):
            b_copy(d).start()

    def relay_b():
        for d in (1, 3, 2):
            b_copy(d).wait_recv()
            r_copy(d).start()

    @pl.when(active)
    def _():
        for which in range(3):
            for g in range(2):
                own_copy(which, g).wait()
        peak_ref[...] = jnp.full_like(peak_ref, FLOOR)
        sum_ref[...] = jnp.zeros_like(sum_ref)
        numer_ref[...] = jnp.zeros_like(numer_ref)
        pass_on(0)
        for d in (1, 3, 2):
            for g in range(2):
                z_copy(0, g, d).wait_recv()

    start_b()

    @pl.when(active)
    def _():
        def step(i, carry):
            before = {
                3: last_row,
                4: lambda: wait_far(0),
                6: lambda: pass_on(1),
                8: lambda: pass_on(3),
                11: lambda: (pass_on(2), wait_far(1)),
                14: lambda: wait_far(3),
                15: lambda: wait_far(2),
            }
            for when, act in before.items():
                @pl.when(i == when)
                def _():
                    act()
            back_z, back_x = 0, 0
            for when, (dz, dx) in enumerate(ORDER):
                back_z = jnp.where(i == when, dz, back_z)
                back_x = jnp.where(i == when, dx, back_x)
            block = mod(zh - back_z, 4) * 4 + mod(x - back_x, 4)
            queries = q_buf[...].reshape(4 * TILE, HD)
            scores = lax.dot_general(
                k_buf[block], queries, (((1,), (1,)), ((), ())), preferred_element_type=jnp.float32
            )
            row = lax.broadcasted_iota(jnp.int32, (TILE, 1), 0)
            back_y = jnp.zeros_like(row)
            for slot, dy in enumerate(SLOTS):
                back_y = jnp.where(row >= slot * ROWS, dy, back_y)
            position = block * TILE + mod(y - back_y, 4) * ROWS + lax.rem(row, ROWS)
            scores = scores + jnp.where(position < limit, 0.0, FLOOR)
            peak = peak_ref[...]
            new_peak = jnp.maximum(peak, jnp.max(scores, axis=0, keepdims=True))
            factor = jnp.exp2(peak - new_peak)
            probs = jnp.exp2(scores - new_peak).astype(jnp.bfloat16)
            with_ones = jnp.concatenate([vt_buf[block], jnp.ones((16, TILE), jnp.bfloat16)], 0)
            mixed = jnp.dot(with_ones, probs, preferred_element_type=jnp.float32)
            peak_ref[...] = new_peak
            sum_ref[...] = sum_ref[...] * factor + mixed[HD : HD + 1]
            numer_ref[...] = numer_ref[...] * factor + mixed[:HD]
            return carry

        lax.fori_loop(0, 16, step, 0)
        attended = numer_ref[...] / sum_ref[...]
        done_buf[...] = attended.T.astype(jnp.bfloat16)
        for dz in (2, 1, 3, 0):
            for slot in (3, 1, 2, 0):
                out_copy(dz, slot).start()

    relay_b()
    for d in (1, 3, 2):
        r_copy(d).wait_recv()

    @pl.when(active)
    def _():
        out_copy(0, 0).wait()

    for dz in range(4):
        @pl.when(head_of(mod(zh - dz, 4)) < HEADS_HERE)
        def _():
            for slot in range(4):
                if dz + slot > 0:
                    out_copy(dz, slot).wait_recv()

    out_proj = jnp.dot(att_buf[...], wo_buf[...], preferred_element_type=jnp.float32)
    out_ref[...] = (x_ref[...].astype(jnp.float32) + mod_ref[2] * out_proj).astype(jnp.bfloat16)

    for i in range(5):
        w_copy(i).wait_send()
        a_copy(i).wait_send()
    for i in range(4):
        y_copy(i).wait_send()
    for d in (1, 3, 2):
        b_copy(d).wait_send()
        r_copy(d).wait_send()
    for which in range(3):
        for g in range(2):
            for d in (1, 3):
                @pl.when(takes(d))
                def _():
                    z_copy(which, g, d).wait_send()

            @pl.when(takes(2))
            def _():
                first_hop(which, g).wait_send()

            @pl.when(head_of(mod(zh + way(which), 4)) < HEADS_HERE)
            def _():
                second_hop(which, g).wait_send()

    @pl.when(active)
    def _():
        for d in range(4):
            for g in range(2):
                for i in range(6):
                    x_copy(d, g, i).wait_send()
        for dz in range(4):
            for slot in range(4):
                if dz + slot > 0:
                    out_copy(dz, slot).wait_send()


def body(hidden_states, modulation, w_qkv, w_out, lengths):
    vmem = pl.BlockSpec(memory_space=pltpu.VMEM)
    dma = pltpu.SemaphoreType.DMA
    bf16 = jnp.bfloat16
    updated = pl.pallas_call(
        kernel,
        name="block",
        out_shape=jax.ShapeDtypeStruct((ROWS, WIDTH), bf16),
        in_specs=[pl.BlockSpec(memory_space=pltpu.SMEM)] + [vmem] * 4,
        out_specs=vmem,
        scratch_shapes=[
            pltpu.VMEM((4, ROWS, WIDTH), bf16),
            pltpu.VMEM((3, WIDTH, PART), bf16),
            pltpu.VMEM((WIDTH, WIDTH), bf16),
            pltpu.VMEM((HEADS_HERE, TILE, HD), bf16),
            pltpu.VMEM((HEADS_HERE, TILE, HD), bf16),
            pltpu.VMEM((HEADS_HERE, HD, TILE), bf16),
            pltpu.VMEM((TILE, HD), bf16),
            pltpu.VMEM((TILE, HD), bf16),
            pltpu.VMEM((HD, TILE), bf16),
            pltpu.VMEM((4, TILE, HD), bf16),
            pltpu.VMEM((16, TILE, HD), bf16),
            pltpu.VMEM((16, HD, TILE), bf16),
            pltpu.VMEM((1, 4 * TILE), jnp.float32),
            pltpu.VMEM((1, 4 * TILE), jnp.float32),
            pltpu.VMEM((HD, 4 * TILE), jnp.float32),
            pltpu.VMEM((4 * TILE, HD), bf16),
            pltpu.VMEM((ROWS, WIDTH), bf16),
            dma((5,)), dma((5,)), dma((5,)), dma((5,)),
            dma((4,)), dma((4,)), dma((4,)), dma((4,)), dma((4,)), dma((4,)),
            dma((6,)), dma((6,)), dma((6, 4)), dma((6, 4)), dma((8, 6)), dma((8, 6)), dma((16,)), dma((16,)), dma((8,)),
        ],
        compiler_params=pltpu.CompilerParams(
            collective_id=0, has_side_effects=True, vmem_limit_bytes=56 << 20
        ),
    )(
        lengths,
        hidden_states[0],
        jnp.transpose(modulation, (1, 0, 2)),
        jnp.transpose(w_qkv, (1, 0, 2)),
        w_out,
    )
    return updated[None]


def solution(mesh):
    placed = (
        P("wrow", ("patch", "wcol"), None),
        P("wrow", None, None),
        P("wrow", None, "wcol"),
        P("wcol", "wrow"),
        P("wrow"),
    )
    return jax.shard_map(
        body,
        mesh=mesh,
        in_specs=placed,
        out_specs=P("wrow", ("patch", "wcol"), None),
        check_vma=False,
    )
```

```python
import math

import jax
import jax.numpy as jnp
from jax import lax
from jax.experimental import pallas as pl
from jax.experimental.pallas import tpu as pltpu
from jax.sharding import PartitionSpec as P

HD = 128
HEADS_HERE = 3
TILE = 512
ROWS = 128
WIDTH = 1536
PART = 384
HALF = PART // 2
EPSILON = 1e-06
FLOOR = -1e30
SCORE_SCALE = HD**-0.5 * math.log2(math.e)
MESH = pl.DeviceIdType.MESH

SLOTS = (0, 1, 3, 2)
HALF_ROWS = ROWS // 2
LAST = 3
SPAN = (slice(0, 3 * ROWS), slice(3 * ROWS, 4 * ROWS))

ORDER = (
    (1, 0), (3, 0), (2, 0), (1, 1), (1, 3), (3, 1),
    (3, 3), (1, 2), (3, 2), (2, 1), (2, 3), (2, 2),
)


def mod(a, n):
    return lax.rem(a + 2 * n, n)


def device(zh, x, zl, core, y):
    return (zh * 4 + x, zl * 2 + core, y)


def remote(src, dst, send_sem, recv_sem, target):
    return pltpu.make_async_remote_copy(
        src_ref=src,
        dst_ref=dst,
        send_sem=send_sem,
        recv_sem=recv_sem,
        device_id=target,
        device_id_type=MESH,
    )


def kernel(
    len_ref, x_ref, mod_ref, w_ref, wo_ref, out_ref,
    rows, weights, wo_buf, q_in, k_in, vt_in,
    rq_buf, rk_buf, rv_buf, q_buf, k_buf, vt_buf, peak_ref, sum_ref, numer_ref, done_buf, att_buf,
    w_send, w_recv, a_send, a_recv, b_send, b_recv, r_send, r_recv, y_send, y_recv,
    h_send, h_recv, z_send, z_recv, x_send, x_recv, o_send, o_recv, own_sem,
):
    patch, video, y = lax.axis_index("patch"), lax.axis_index("wrow"), lax.axis_index("wcol")
    zh, x = patch // 4, lax.rem(patch, 4)
    zl, core = video // 2, lax.rem(video, 2)
    z = zh * 2 + zl
    limit = len_ref[0]

    def at(dzh=0, dx=0, dy=0):
        return device(mod(zh + dzh, 4), mod(x + dx, 4), zl, core, mod(y + dy, 4))

    up_z, down_z = mod(z + 1, 8), mod(z - 1, 8)
    up = device(up_z // 2, x, lax.rem(up_z, 2), core, y)
    down = device(down_z // 2, x, lax.rem(down_z, 2), core, y)
    partner = device(zh, x, zl, 1 - core, y)
    right, left = at(dx=1), at(dx=-1)

    barrier = pltpu.get_barrier_semaphore()
    targets = [up, down, partner, right, left]
    targets += [at(dzh=dz, dy=dy) for dz in range(4) for dy in range(4) if dz + dy > 0]
    for target in targets:
        pl.semaphore_signal(barrier, inc=1, device_id=target, device_id_type=MESH)
    pl.semaphore_wait(barrier, len(targets))

    mine_first = pl.multiple_of(video * PART, PART)
    theirs_first = pl.multiple_of(((1 - zl) * 2 + core) * PART, PART)

    def w_copy(i):
        if i == 0:
            src, first, count, target = w_ref.at[:, pl.ds(HALF, HALF)], mine_first + HALF, HALF, up
        elif i == 1:
            src, first, count, target = w_ref.at[:, pl.ds(0, HALF)], mine_first, HALF, down
        elif i == 2:
            src, first, count, target = w_ref, mine_first, PART, partner
        else:
            first, count, target = theirs_first + (HALF if i == 3 else 0), HALF, partner
            src = weights.at[:, pl.ds(first, count)]
        return remote(src, weights.at[:, pl.ds(first, count)], w_send.at[i], w_recv.at[i], target)

    wo_rows = pl.multiple_of(y * PART, PART)

    def a_copy(i):
        first = wo_rows + (HALF if i in (0, 3) else 0)
        count = PART if i == 2 else HALF
        column = mine_first if i < 3 else theirs_first
        target = (up, down, partner, partner, partner)[i]
        src = wo_buf.at[pl.ds(first, count), pl.ds(column, PART)]
        return remote(src, src, a_send.at[i], a_recv.at[i], target)

    def b_copy(d):
        part = wo_buf.at[pl.ds(wo_rows + core * HALF, HALF)]
        return remote(part, part, b_send.at[d], b_recv.at[d], at(dy=d))

    def r_copy(d):
        part = wo_buf.at[pl.ds(mod(y - d, 4) * PART + core * HALF, HALF)]
        return remote(part, part, r_send.at[d], r_recv.at[d], partner)

    def own_w():
        return pltpu.make_async_copy(w_ref, weights.at[:, pl.ds(mine_first, PART)], own_sem.at[6])

    def own_wo():
        return pltpu.make_async_copy(
            wo_ref, wo_buf.at[pl.ds(wo_rows, PART), pl.ds(mine_first, PART)], own_sem.at[7]
        )

    def y_copy(i):
        src = rows.at[0] if i < 2 else rows.at[i - 1, pl.ds((i - 2) * HALF_ROWS, HALF_ROWS)]
        dst = rows.at[1 + i] if i < 2 else rows.at[3, pl.ds((i - 2) * HALF_ROWS, HALF_ROWS)]
        target = at(dy=1) if i in (0, 2) else at(dy=-1)
        return remote(src, dst, y_send.at[i], y_recv.at[i], target)

    for i in (0, 1, 2):
        w_copy(i).start()
    own_w().start()
    own_wo().start()

    values = x_ref[...].astype(jnp.float32)
    center = jnp.mean(values, axis=-1, keepdims=True)
    values = values - center
    spread = jnp.mean(jnp.square(values), axis=-1, keepdims=True)
    normed = values * lax.rsqrt(spread + EPSILON) * (1.0 + mod_ref[1]) + mod_ref[0]
    rows[0] = normed.astype(jnp.bfloat16)
    for i in (0, 1):
        y_copy(i).start()

    for i in (0, 1):
        w_copy(i).wait_recv()
        w_copy(3 + i).start()
    for i in (0, 1):
        y_copy(i).wait_recv()
        y_copy(2 + i).start()
    own_w().wait()
    for i in (2, 3, 4):
        w_copy(i).wait_recv()

    idle = lax.rem(video, 2) * 2 + video // 2

    def head_of(row):
        return mod(row - idle - 1, 4)

    head = head_of(zh)
    active = head < HEADS_HERE
    head = jnp.minimum(head, HEADS_HERE - 1)
    own_block = zh * 4 + x

    def cut(ref, which, g):
        return ref.at[:, SPAN[g]] if which == 2 else ref.at[SPAN[g]]

    z_in, z_buf = (q_in, k_in, vt_in), (q_buf, k_buf, vt_buf)
    turn = 1 - 2 * core

    def takes(d):
        return head_of(mod(zh + d, 4)) < HEADS_HERE

    def tile_index(which, row):
        return row if which == 0 else row * 4 + x

    def z_copy(which, g, d):
        there = jnp.minimum(head_of(mod(zh + d, 4)), HEADS_HERE - 1)
        return remote(
            cut(z_in[which].at[there], which, g),
            cut(z_buf[which].at[tile_index(which, zh)], which, g),
            z_send.at[which * 2 + g, d],
            z_recv.at[which * 2 + g, d],
            at(dzh=d),
        )

    def way(which):
        return -turn if which == 2 else turn

    def first_hop(which, g):
        there = jnp.minimum(head_of(mod(zh + 2, 4)), HEADS_HERE - 1)
        return remote(
            cut(z_in[which].at[there], which, g),
            cut((rq_buf, rk_buf, rv_buf)[which], which, g),
            h_send.at[which * 2 + g],
            h_recv.at[which * 2 + g],
            at(dzh=way(which)),
        )

    def second_hop(which, g):
        source = mod(zh - way(which), 4)
        return remote(
            cut((rq_buf, rk_buf, rv_buf)[which], which, g),
            cut(z_buf[which].at[tile_index(which, source)], which, g),
            z_send.at[which * 2 + g, 2],
            z_recv.at[which * 2 + g, 2],
            at(dzh=way(which)),
        )

    def own_copy(which, g):
        return pltpu.make_async_copy(
            cut(z_in[which].at[head], which, g),
            cut(z_buf[which].at[tile_index(which, zh)], which, g),
            own_sem.at[which * 2 + g],
        )

    def x_copy(d, g, i):
        source = mod(zh - d, 4)
        column = (x, x, x, x, mod(x - 1, 4), mod(x + 1, 4))[i]
        which = 1 + i % 2
        target = (right, right, left, left, right, left)[i]
        block = source * 4 + column
        dst = cut(z_buf[which].at[block], which, g)
        src = cut(z_in[which].at[head], which, g) if d == 0 and i < 4 else dst
        return remote(src, dst, x_send.at[d * 2 + g, i], x_recv.at[d * 2 + g, i], target)

    def spread_out(d, g):
        for i in range(4):
            x_copy(d, g, i).start()

    def project(g, first, count):
        flat = rows[pl.ds(first, count)].reshape(count * ROWS, WIDTH)
        for which in range(3):
            part = jnp.dot(flat, weights[which], preferred_element_type=jnp.float32)
            if which == 0:
                part = part * SCORE_SCALE
            for h in range(HEADS_HERE):
                one = part[:, h * HD : (h + 1) * HD]
                if which == 2:
                    vt_in[h, :, SPAN[g]] = one.T.astype(jnp.bfloat16)
                else:
                    z_in[which][h, SPAN[g]] = one.astype(jnp.bfloat16)

            @pl.when(takes(2))
            def _():
                first_hop(which, g).start()

            for d in (1, 3):
                @pl.when(takes(d))
                def _():
                    z_copy(which, g, d).start()

            @pl.when(active)
            def _():
                own_copy(which, g).start()

        @pl.when(active)
        def _():
            spread_out(0, g)

    def relay(g):
        for which in range(3):
            @pl.when(head_of(mod(zh + way(which), 4)) < HEADS_HERE)
            def _():
                first_hop(which, g).wait_recv()
                second_hop(which, g).start()

    def wait_z(d, g):
        z_copy(1, g, d).wait_recv()
        z_copy(2, g, d).wait_recv()

    project(0, 0, 3)
    for i in (2, 3):
        y_copy(i).wait_recv()
    project(1, 3, 1)
    own_wo().wait()
    for i in (0, 1, 2):
        a_copy(i).start()
    relay(0)

    @pl.when(active)
    def _():
        for d in (1, 3):
            wait_z(d, 0)
            spread_out(d, 0)

    def pass_on(d):
        for g in range(2):
            for i in range(4):
                x_copy(d, g, i).wait_recv()
            x_copy(d, g, 4).start()
            x_copy(d, g, 5).start()

    def wait_far(d):
        for g in range(2):
            x_copy(d, g, 4).wait_recv()
            x_copy(d, g, 5).wait_recv()

    @pl.when(active)
    def _():
        pass_on(0)

    relay(1)

    @pl.when(active)
    def _():
        for d in (1, 3):
            wait_z(d, 1)
            spread_out(d, 1)

    for i in (0, 1):
        a_copy(i).wait_recv()
        a_copy(3 + i).start()

    def last_row():
        for g in range(2):
            wait_z(2, g)
            spread_out(2, g)

    def out_copy(dz, slot):
        first = pl.multiple_of(mod(zh + dz, 4) * TILE + slot * ROWS, ROWS)
        column = pl.multiple_of((y * HEADS_HERE + head) * HD, HD)
        i = dz * 4 + slot
        src = done_buf.at[pl.ds(first, ROWS)]
        dst = att_buf.at[:, pl.ds(column, HD)]
        if i == 0:
            return pltpu.make_async_copy(src, dst, o_send.at[0])
        return remote(src, dst, o_send.at[i], o_recv.at[i], at(dzh=dz, dy=-SLOTS[slot]))

    def start_b():
        for i in (2, 3, 4):
            a_copy(i).wait_recv()
        for d in (1, 3, 2):
            b_copy(d).start()

    def relay_b():
        for d in (1, 3, 2):
            b_copy(d).wait_recv()
            r_copy(d).start()

    @pl.when(active)
    def _():
        for which in range(3):
            for g in range(2):
                own_copy(which, g).wait()
        peak_ref[...] = jnp.full_like(peak_ref, FLOOR)
        sum_ref[...] = jnp.zeros_like(sum_ref)
        numer_ref[...] = jnp.zeros_like(numer_ref)

    start_b()

    @pl.when(active)
    def _():
        def block_at(back_z, back_x):
            return mod(zh - back_z, 4) * 4 + mod(x - back_x, 4)

        def bias(block):
            row = lax.broadcasted_iota(jnp.int32, (TILE, 1), 0)
            back_y = jnp.zeros_like(row)
            for slot, dy in enumerate(SLOTS):
                back_y = jnp.where(row >= slot * ROWS, dy, back_y)
            position = block * TILE + mod(y - back_y, 4) * ROWS + lax.rem(row, ROWS)
            return jnp.where(position < limit, 0.0, FLOOR)

        def absorb(blocks, queries, peak, total, numer):
            scores = []
            for block in blocks:
                one = lax.dot_general(
                    k_buf[block], queries, (((1,), (1,)), ((), ())), preferred_element_type=jnp.float32
                )
                scores.append(one + bias(block))
            new_peak = peak
            for one in scores:
                new_peak = jnp.maximum(new_peak, jnp.max(one, axis=0, keepdims=True))
            factor = jnp.exp2(peak - new_peak)
            total, numer = total * factor, numer * factor
            for block, one in zip(blocks, scores):
                probs = jnp.exp2(one - new_peak).astype(jnp.bfloat16)
                with_ones = jnp.concatenate([vt_buf[block], jnp.ones((16, TILE), jnp.bfloat16)], 0)
                mixed = jnp.dot(with_ones, probs, preferred_element_type=jnp.float32)
                total, numer = total + mixed[HD : HD + 1], numer + mixed[:HD]
            return new_peak, total, numer

        wait_far(0)
        near_blocks = [block_at(0, dx) for dx in (0, 1, 3, 2)]

        def own_row(i, carry):
            for when, d in ((1, 1), (2, 3), (3, 2)):
                @pl.when(i == when)
                def _():
                    if d == 2:
                        last_row()
                    for g in range(2):
                        z_copy(0, g, d).wait_recv()
            back = jnp.where(i == 1, 1, jnp.where(i == 2, 3, jnp.where(i == 3, 2, 0)))
            tile = mod(zh - back, 4)
            columns = pl.ds(pl.multiple_of(tile * TILE, TILE), TILE)
            peak_ref[:, columns], sum_ref[:, columns], numer_ref[:, columns] = absorb(
                near_blocks, q_buf[tile], peak_ref[:, columns], sum_ref[:, columns], numer_ref[:, columns]
            )
            return carry

        lax.fori_loop(0, 4, own_row, 0)
        before = {
            1: lambda: pass_on(1),
            2: lambda: pass_on(3),
            4: lambda: pass_on(2),
            7: lambda: wait_far(1),
            8: lambda: wait_far(3),
            9: lambda: wait_far(2),
        }

        def step(i, carry):
            for when, act in before.items():
                if when < 12 - LAST:
                    @pl.when(i == when)
                    def _():
                        act()
            back_z, back_x = 0, 0
            for when, (dz, dx) in enumerate(ORDER):
                back_z = jnp.where(i == when, dz, back_z)
                back_x = jnp.where(i == when, dx, back_x)
            queries = q_buf[...].reshape(4 * TILE, HD)
            peak_ref[...], sum_ref[...], numer_ref[...] = absorb(
                [block_at(back_z, back_x)], queries, peak_ref[...], sum_ref[...], numer_ref[...]
            )
            return carry

        lax.fori_loop(0, 12 - LAST, step, 0)
        for when, act in before.items():
            if when >= 12 - LAST:
                act()

        blocks = [block_at(*back) for back in ORDER[12 - LAST :]]
        for dz in (2, 1, 3, 0):
            tile = mod(zh + dz, 4)
            columns = pl.ds(pl.multiple_of(tile * TILE, TILE), TILE)
            _, total, numer = absorb(
                blocks, q_buf[tile], peak_ref[:, columns], sum_ref[:, columns], numer_ref[:, columns]
            )
            done_buf[columns] = (numer / total).T.astype(jnp.bfloat16)
            for slot in (3, 1, 2, 0):
                out_copy(dz, slot).start()

    relay_b()
    for d in (1, 3, 2):
        r_copy(d).wait_recv()

    @pl.when(active)
    def _():
        out_copy(0, 0).wait()

    for dz in range(4):
        @pl.when(head_of(mod(zh - dz, 4)) < HEADS_HERE)
        def _():
            for slot in range(4):
                if dz + slot > 0:
                    out_copy(dz, slot).wait_recv()

    out_proj = jnp.dot(att_buf[...], wo_buf[...], preferred_element_type=jnp.float32)
    out_ref[...] = (x_ref[...].astype(jnp.float32) + mod_ref[2] * out_proj).astype(jnp.bfloat16)

    for i in range(5):
        w_copy(i).wait_send()
        a_copy(i).wait_send()
    for i in range(4):
        y_copy(i).wait_send()
    for d in (1, 3, 2):
        b_copy(d).wait_send()
        r_copy(d).wait_send()
    for which in range(3):
        for g in range(2):
            for d in (1, 3):
                @pl.when(takes(d))
                def _():
                    z_copy(which, g, d).wait_send()

            @pl.when(takes(2))
            def _():
                first_hop(which, g).wait_send()

            @pl.when(head_of(mod(zh + way(which), 4)) < HEADS_HERE)
            def _():
                second_hop(which, g).wait_send()

    @pl.when(active)
    def _():
        for d in range(4):
            for g in range(2):
                for i in range(6):
                    x_copy(d, g, i).wait_send()
        for dz in range(4):
            for slot in range(4):
                if dz + slot > 0:
                    out_copy(dz, slot).wait_send()


def body(hidden_states, modulation, w_qkv, w_out, lengths):
    vmem = pl.BlockSpec(memory_space=pltpu.VMEM)
    dma = pltpu.SemaphoreType.DMA
    bf16 = jnp.bfloat16
    updated = pl.pallas_call(
        kernel,
        name="block",
        out_shape=jax.ShapeDtypeStruct((ROWS, WIDTH), bf16),
        in_specs=[pl.BlockSpec(memory_space=pltpu.SMEM)] + [vmem] * 4,
        out_specs=vmem,
        scratch_shapes=[
            pltpu.VMEM((4, ROWS, WIDTH), bf16),
            pltpu.VMEM((3, WIDTH, PART), bf16),
            pltpu.VMEM((WIDTH, WIDTH), bf16),
            pltpu.VMEM((HEADS_HERE, TILE, HD), bf16),
            pltpu.VMEM((HEADS_HERE, TILE, HD), bf16),
            pltpu.VMEM((HEADS_HERE, HD, TILE), bf16),
            pltpu.VMEM((TILE, HD), bf16),
            pltpu.VMEM((TILE, HD), bf16),
            pltpu.VMEM((HD, TILE), bf16),
            pltpu.VMEM((4, TILE, HD), bf16),
            pltpu.VMEM((16, TILE, HD), bf16),
            pltpu.VMEM((16, HD, TILE), bf16),
            pltpu.VMEM((1, 4 * TILE), jnp.float32),
            pltpu.VMEM((1, 4 * TILE), jnp.float32),
            pltpu.VMEM((HD, 4 * TILE), jnp.float32),
            pltpu.VMEM((4 * TILE, HD), bf16),
            pltpu.VMEM((ROWS, WIDTH), bf16),
            dma((5,)), dma((5,)), dma((5,)), dma((5,)),
            dma((4,)), dma((4,)), dma((4,)), dma((4,)), dma((4,)), dma((4,)),
            dma((6,)), dma((6,)), dma((6, 4)), dma((6, 4)), dma((8, 6)), dma((8, 6)), dma((16,)), dma((16,)), dma((8,)),
        ],
        compiler_params=pltpu.CompilerParams(
            collective_id=0, has_side_effects=True, vmem_limit_bytes=56 << 20
        ),
    )(
        lengths,
        hidden_states[0],
        jnp.transpose(modulation, (1, 0, 2)),
        jnp.transpose(w_qkv, (1, 0, 2)),
        w_out,
    )
    return updated[None]


def solution(mesh):
    placed = (
        P("wrow", ("patch", "wcol"), None),
        P("wrow", None, None),
        P("wrow", None, "wcol"),
        P("wcol", "wrow"),
        P("wrow"),
    )
    return jax.shard_map(
        body,
        mesh=mesh,
        in_specs=placed,
        out_specs=P("wrow", ("patch", "wcol"), None),
        check_vma=False,
    )
```

```python
import math

import jax
import jax.numpy as jnp
from jax import lax
from jax.experimental import pallas as pl
from jax.experimental.pallas import tpu as pltpu
from jax.sharding import PartitionSpec as P

HD = 128
HEADS_HERE = 3
TILE = 512
ROWS = 128
WIDTH = 1536
PART = 384
HALF = PART // 2
EPSILON = 1e-06
FLOOR = -1e30
SCORE_SCALE = HD**-0.5 * math.log2(math.e)
MESH = pl.DeviceIdType.MESH

SLOTS = (0, 1, 3, 2)
HALF_ROWS = ROWS // 2
LAST = 3
SPAN = (slice(0, 3 * ROWS), slice(3 * ROWS, 4 * ROWS))

ORDER = (
    (1, 0), (3, 0), (2, 0), (1, 1), (1, 3), (3, 1),
    (3, 3), (1, 2), (3, 2), (2, 1), (2, 3), (2, 2),
)


def mod(a, n):
    return lax.rem(a + 2 * n, n)


def device(zh, x, zl, core, y):
    return (zh * 4 + x, zl * 2 + core, y)


def remote(src, dst, send_sem, recv_sem, target):
    return pltpu.make_async_remote_copy(
        src_ref=src,
        dst_ref=dst,
        send_sem=send_sem,
        recv_sem=recv_sem,
        device_id=target,
        device_id_type=MESH,
    )


def kernel(
    len_ref, x_ref, mod_ref, w_ref, wo_ref, out_ref,
    rows, weights, wo_buf, q_in, k_in, vt_in,
    rq_buf, rk_buf, rv_buf, q_buf, k_buf, vt_buf, peak_ref, sum_ref, numer_ref, done_buf, att_buf,
    w_send, w_recv, a_send, a_recv, b_send, b_recv, r_send, r_recv, y_send, y_recv,
    h_send, h_recv, z_send, z_recv, x_send, x_recv, o_send, o_recv, own_sem,
):
    patch, video, y = lax.axis_index("patch"), lax.axis_index("wrow"), lax.axis_index("wcol")
    zh, x = patch // 4, lax.rem(patch, 4)
    zl, core = video // 2, lax.rem(video, 2)
    z = zh * 2 + zl
    limit = len_ref[0]

    def at(dzh=0, dx=0, dy=0):
        return device(mod(zh + dzh, 4), mod(x + dx, 4), zl, core, mod(y + dy, 4))

    up_z, down_z = mod(z + 1, 8), mod(z - 1, 8)
    up = device(up_z // 2, x, lax.rem(up_z, 2), core, y)
    down = device(down_z // 2, x, lax.rem(down_z, 2), core, y)
    partner = device(zh, x, zl, 1 - core, y)
    right, left = at(dx=1), at(dx=-1)

    barrier = pltpu.get_barrier_semaphore()
    targets = [up, down, partner, right, left]
    targets += [at(dzh=dz, dy=dy) for dz in range(4) for dy in range(4) if dz + dy > 0]
    for target in targets:
        pl.semaphore_signal(barrier, inc=1, device_id=target, device_id_type=MESH)
    pl.semaphore_wait(barrier, len(targets))

    mine_first = pl.multiple_of(video * PART, PART)
    theirs_first = pl.multiple_of(((1 - zl) * 2 + core) * PART, PART)

    def w_copy(i):
        if i == 0:
            src, first, count, target = w_ref.at[:, pl.ds(HALF, HALF)], mine_first + HALF, HALF, up
        elif i == 1:
            src, first, count, target = w_ref.at[:, pl.ds(0, HALF)], mine_first, HALF, down
        elif i == 2:
            src, first, count, target = w_ref, mine_first, PART, partner
        else:
            first, count, target = theirs_first + (HALF if i == 3 else 0), HALF, partner
            src = weights.at[:, pl.ds(first, count)]
        return remote(src, weights.at[:, pl.ds(first, count)], w_send.at[i], w_recv.at[i], target)

    wo_rows = pl.multiple_of(y * PART, PART)

    def a_copy(i):
        first = wo_rows + (HALF if i in (0, 3) else 0)
        count = PART if i == 2 else HALF
        column = mine_first if i < 3 else theirs_first
        target = (up, down, partner, partner, partner)[i]
        src = wo_buf.at[pl.ds(first, count), pl.ds(column, PART)]
        return remote(src, src, a_send.at[i], a_recv.at[i], target)

    def b_copy(d):
        part = wo_buf.at[pl.ds(wo_rows + core * HALF, HALF)]
        return remote(part, part, b_send.at[d], b_recv.at[d], at(dy=d))

    def r_copy(d):
        part = wo_buf.at[pl.ds(mod(y - d, 4) * PART + core * HALF, HALF)]
        return remote(part, part, r_send.at[d], r_recv.at[d], partner)

    def own_w():
        return pltpu.make_async_copy(w_ref, weights.at[:, pl.ds(mine_first, PART)], own_sem.at[6])

    def own_wo():
        return pltpu.make_async_copy(
            wo_ref, wo_buf.at[pl.ds(wo_rows, PART), pl.ds(mine_first, PART)], own_sem.at[7]
        )

    def y_copy(i):
        src = rows.at[0] if i < 2 else rows.at[i - 1, pl.ds((i - 2) * HALF_ROWS, HALF_ROWS)]
        dst = rows.at[1 + i] if i < 2 else rows.at[3, pl.ds((i - 2) * HALF_ROWS, HALF_ROWS)]
        target = at(dy=1) if i in (0, 2) else at(dy=-1)
        return remote(src, dst, y_send.at[i], y_recv.at[i], target)

    for i in (0, 1, 2):
        w_copy(i).start()
    own_w().start()
    own_wo().start()

    values = x_ref[...].astype(jnp.float32)
    center = jnp.mean(values, axis=-1, keepdims=True)
    values = values - center
    spread = jnp.mean(jnp.square(values), axis=-1, keepdims=True)
    normed = values * lax.rsqrt(spread + EPSILON) * (1.0 + mod_ref[1]) + mod_ref[0]
    rows[0] = normed.astype(jnp.bfloat16)
    for i in (0, 1):
        y_copy(i).start()

    for i in (0, 1):
        w_copy(i).wait_recv()
        w_copy(3 + i).start()
    for i in (0, 1):
        y_copy(i).wait_recv()
        y_copy(2 + i).start()
    own_w().wait()
    for i in (2, 3, 4):
        w_copy(i).wait_recv()

    idle = lax.rem(video, 2) * 2 + video // 2

    def head_of(row):
        return mod(row - idle - 1, 4)

    head = head_of(zh)
    active = head < HEADS_HERE
    head = jnp.minimum(head, HEADS_HERE - 1)
    own_block = zh * 4 + x

    def cut(ref, which, g):
        return ref.at[:, SPAN[g]] if which == 2 else ref.at[SPAN[g]]

    z_in, z_buf = (q_in, k_in, vt_in), (q_buf, k_buf, vt_buf)
    turn = 1 - 2 * core

    def takes(d):
        return head_of(mod(zh + d, 4)) < HEADS_HERE

    def tile_index(which, row):
        return row if which == 0 else row * 4 + x

    def z_copy(which, g, d):
        there = jnp.minimum(head_of(mod(zh + d, 4)), HEADS_HERE - 1)
        return remote(
            cut(z_in[which].at[there], which, g),
            cut(z_buf[which].at[tile_index(which, zh)], which, g),
            z_send.at[which * 2 + g, d],
            z_recv.at[which * 2 + g, d],
            at(dzh=d),
        )

    def way(which):
        return -turn if which == 2 else turn

    def first_hop(which, g):
        there = jnp.minimum(head_of(mod(zh + 2, 4)), HEADS_HERE - 1)
        return remote(
            cut(z_in[which].at[there], which, g),
            cut((rq_buf, rk_buf, rv_buf)[which], which, g),
            h_send.at[which * 2 + g],
            h_recv.at[which * 2 + g],
            at(dzh=way(which)),
        )

    def second_hop(which, g):
        source = mod(zh - way(which), 4)
        return remote(
            cut((rq_buf, rk_buf, rv_buf)[which], which, g),
            cut(z_buf[which].at[tile_index(which, source)], which, g),
            z_send.at[which * 2 + g, 2],
            z_recv.at[which * 2 + g, 2],
            at(dzh=way(which)),
        )

    def own_copy(which, g):
        return pltpu.make_async_copy(
            cut(z_in[which].at[head], which, g),
            cut(z_buf[which].at[tile_index(which, zh)], which, g),
            own_sem.at[which * 2 + g],
        )

    def x_copy(d, g, i):
        source = mod(zh - d, 4)
        column = (x, x, x, x, mod(x - 1, 4), mod(x + 1, 4))[i]
        which = 1 + i % 2
        target = (right, right, left, left, right, left)[i]
        block = source * 4 + column
        dst = cut(z_buf[which].at[block], which, g)
        src = cut(z_in[which].at[head], which, g) if d == 0 and i < 4 else dst
        return remote(src, dst, x_send.at[d * 2 + g, i], x_recv.at[d * 2 + g, i], target)

    def spread_out(d, g):
        for i in range(4):
            x_copy(d, g, i).start()

    def project(g, first, count):
        flat = rows[pl.ds(first, count)].reshape(count * ROWS, WIDTH)
        for which in range(3):
            part = jnp.dot(flat, weights[which], preferred_element_type=jnp.float32)
            if which == 0:
                part = part * SCORE_SCALE
            for h in range(HEADS_HERE):
                one = part[:, h * HD : (h + 1) * HD]
                if which == 2:
                    vt_in[h, :, SPAN[g]] = one.T.astype(jnp.bfloat16)
                else:
                    z_in[which][h, SPAN[g]] = one.astype(jnp.bfloat16)

            @pl.when(takes(2))
            def _():
                first_hop(which, g).start()

            for d in (1, 3):
                @pl.when(takes(d))
                def _():
                    z_copy(which, g, d).start()

            @pl.when(active)
            def _():
                own_copy(which, g).start()

        @pl.when(active)
        def _():
            spread_out(0, g)

    def relay(g):
        for which in range(3):
            @pl.when(head_of(mod(zh + way(which), 4)) < HEADS_HERE)
            def _():
                first_hop(which, g).wait_recv()
                second_hop(which, g).start()

    def wait_z(d, g):
        z_copy(1, g, d).wait_recv()
        z_copy(2, g, d).wait_recv()

    project(0, 0, 3)
    for i in (2, 3):
        y_copy(i).wait_recv()
    project(1, 3, 1)
    own_wo().wait()
    for i in (0, 1, 2):
        a_copy(i).start()
    relay(0)

    @pl.when(active)
    def _():
        for d in (1, 3):
            wait_z(d, 0)
            spread_out(d, 0)

    def pass_on(d):
        for g in range(2):
            for i in range(4):
                x_copy(d, g, i).wait_recv()
            x_copy(d, g, 4).start()
            x_copy(d, g, 5).start()

    def wait_far(d):
        for g in range(2):
            x_copy(d, g, 4).wait_recv()
            x_copy(d, g, 5).wait_recv()

    @pl.when(active)
    def _():
        pass_on(0)

    relay(1)

    @pl.when(active)
    def _():
        for d in (1, 3):
            wait_z(d, 1)
            spread_out(d, 1)

    for i in (0, 1):
        a_copy(i).wait_recv()
        a_copy(3 + i).start()

    def last_row():
        for g in range(2):
            wait_z(2, g)
            spread_out(2, g)

    def out_copy(dz, slot):
        first = pl.multiple_of(mod(zh + dz, 4) * TILE + slot * ROWS, ROWS)
        column = pl.multiple_of((y * HEADS_HERE + head) * HD, HD)
        i = dz * 4 + slot
        src = done_buf.at[pl.ds(first, ROWS)]
        dst = att_buf.at[:, pl.ds(column, HD)]
        if i == 0:
            return pltpu.make_async_copy(src, dst, o_send.at[0])
        return remote(src, dst, o_send.at[i], o_recv.at[i], at(dzh=dz, dy=-SLOTS[slot]))

    def start_b():
        for i in (2, 3, 4):
            a_copy(i).wait_recv()
        for d in (1, 3, 2):
            b_copy(d).start()

    def relay_b():
        for d in (1, 3, 2):
            b_copy(d).wait_recv()
            r_copy(d).start()

    @pl.when(active)
    def _():
        for which in range(3):
            for g in range(2):
                own_copy(which, g).wait()
        peak_ref[...] = jnp.full_like(peak_ref, FLOOR)
        sum_ref[...] = jnp.zeros_like(sum_ref)
        numer_ref[...] = jnp.zeros_like(numer_ref)

    start_b()

    @pl.when(active)
    def _():
        def block_at(back_z, back_x):
            return mod(zh - back_z, 4) * 4 + mod(x - back_x, 4)

        def bias(block):
            row = lax.broadcasted_iota(jnp.int32, (TILE, 1), 0)
            back_y = jnp.zeros_like(row)
            for slot, dy in enumerate(SLOTS):
                back_y = jnp.where(row >= slot * ROWS, dy, back_y)
            position = block * TILE + mod(y - back_y, 4) * ROWS + lax.rem(row, ROWS)
            return jnp.where(position < limit, 0.0, FLOOR)

        def absorb(blocks, queries, peak, total, numer):
            scores = []
            for block in blocks:
                one = lax.dot_general(
                    k_buf[block], queries, (((1,), (1,)), ((), ())), preferred_element_type=jnp.float32
                )
                scores.append(one + bias(block))
            new_peak = peak
            for one in scores:
                new_peak = jnp.maximum(new_peak, jnp.max(one, axis=0, keepdims=True))
            factor = jnp.exp2(peak - new_peak)
            total, numer = total * factor, numer * factor
            for block, one in zip(blocks, scores):
                probs = jnp.exp2(one - new_peak).astype(jnp.bfloat16)
                with_ones = jnp.concatenate([vt_buf[block], jnp.ones((16, TILE), jnp.bfloat16)], 0)
                mixed = jnp.dot(with_ones, probs, preferred_element_type=jnp.float32)
                total, numer = total + mixed[HD : HD + 1], numer + mixed[:HD]
            return new_peak, total, numer

        wait_far(0)
        near_blocks = [block_at(0, dx) for dx in (0, 1, 3, 2)]

        def own_row(i, carry):
            for when, d in ((1, 1), (2, 3), (3, 2)):
                @pl.when(i == when)
                def _():
                    if d == 3:
                        last_row()
                    for g in range(2):
                        z_copy(0, g, d).wait_recv()
            back = jnp.where(i == 1, 1, jnp.where(i == 2, 3, jnp.where(i == 3, 2, 0)))
            tile = mod(zh - back, 4)
            columns = pl.ds(pl.multiple_of(tile * TILE, TILE), TILE)
            peak_ref[:, columns], sum_ref[:, columns], numer_ref[:, columns] = absorb(
                near_blocks, q_buf[tile], peak_ref[:, columns], sum_ref[:, columns], numer_ref[:, columns]
            )
            return carry

        lax.fori_loop(0, 4, own_row, 0)
        before = {
            0: lambda: pass_on(1),
            1: lambda: pass_on(3),
            3: lambda: pass_on(2),
            7: lambda: wait_far(1),
            8: lambda: wait_far(3),
            9: lambda: wait_far(2),
        }

        def step(i, carry):
            for when, act in before.items():
                if when < 12 - LAST:
                    @pl.when(i == when)
                    def _():
                        act()
            back_z, back_x = 0, 0
            for when, (dz, dx) in enumerate(ORDER):
                back_z = jnp.where(i == when, dz, back_z)
                back_x = jnp.where(i == when, dx, back_x)
            queries = q_buf[...].reshape(4 * TILE, HD)
            peak_ref[...], sum_ref[...], numer_ref[...] = absorb(
                [block_at(back_z, back_x)], queries, peak_ref[...], sum_ref[...], numer_ref[...]
            )
            return carry

        lax.fori_loop(0, 12 - LAST, step, 0)
        for when, act in before.items():
            if when >= 12 - LAST:
                act()

        blocks = [block_at(*back) for back in ORDER[12 - LAST :]]
        for dz in (2, 1, 3, 0):
            tile = mod(zh + dz, 4)
            columns = pl.ds(pl.multiple_of(tile * TILE, TILE), TILE)
            _, total, numer = absorb(
                blocks, q_buf[tile], peak_ref[:, columns], sum_ref[:, columns], numer_ref[:, columns]
            )
            done_buf[columns] = (numer / total).T.astype(jnp.bfloat16)
            for slot in (3, 1, 2, 0):
                out_copy(dz, slot).start()

    relay_b()
    for d in (1, 3, 2):
        r_copy(d).wait_recv()

    @pl.when(active)
    def _():
        out_copy(0, 0).wait()

    for dz in range(4):
        @pl.when(head_of(mod(zh - dz, 4)) < HEADS_HERE)
        def _():
            for slot in range(4):
                if dz + slot > 0:
                    out_copy(dz, slot).wait_recv()

    out_proj = jnp.dot(att_buf[...], wo_buf[...], preferred_element_type=jnp.float32)
    out_ref[...] = (x_ref[...].astype(jnp.float32) + mod_ref[2] * out_proj).astype(jnp.bfloat16)

    for i in range(5):
        w_copy(i).wait_send()
        a_copy(i).wait_send()
    for i in range(4):
        y_copy(i).wait_send()
    for d in (1, 3, 2):
        b_copy(d).wait_send()
        r_copy(d).wait_send()
    for which in range(3):
        for g in range(2):
            for d in (1, 3):
                @pl.when(takes(d))
                def _():
                    z_copy(which, g, d).wait_send()

            @pl.when(takes(2))
            def _():
                first_hop(which, g).wait_send()

            @pl.when(head_of(mod(zh + way(which), 4)) < HEADS_HERE)
            def _():
                second_hop(which, g).wait_send()

    @pl.when(active)
    def _():
        for d in range(4):
            for g in range(2):
                for i in range(6):
                    x_copy(d, g, i).wait_send()
        for dz in range(4):
            for slot in range(4):
                if dz + slot > 0:
                    out_copy(dz, slot).wait_send()


def body(hidden_states, modulation, w_qkv, w_out, lengths):
    vmem = pl.BlockSpec(memory_space=pltpu.VMEM)
    dma = pltpu.SemaphoreType.DMA
    bf16 = jnp.bfloat16
    updated = pl.pallas_call(
        kernel,
        name="block",
        out_shape=jax.ShapeDtypeStruct((ROWS, WIDTH), bf16),
        in_specs=[pl.BlockSpec(memory_space=pltpu.SMEM)] + [vmem] * 4,
        out_specs=vmem,
        scratch_shapes=[
            pltpu.VMEM((4, ROWS, WIDTH), bf16),
            pltpu.VMEM((3, WIDTH, PART), bf16),
            pltpu.VMEM((WIDTH, WIDTH), bf16),
            pltpu.VMEM((HEADS_HERE, TILE, HD), bf16),
            pltpu.VMEM((HEADS_HERE, TILE, HD), bf16),
            pltpu.VMEM((HEADS_HERE, HD, TILE), bf16),
            pltpu.VMEM((TILE, HD), bf16),
            pltpu.VMEM((TILE, HD), bf16),
            pltpu.VMEM((HD, TILE), bf16),
            pltpu.VMEM((4, TILE, HD), bf16),
            pltpu.VMEM((16, TILE, HD), bf16),
            pltpu.VMEM((16, HD, TILE), bf16),
            pltpu.VMEM((1, 4 * TILE), jnp.float32),
            pltpu.VMEM((1, 4 * TILE), jnp.float32),
            pltpu.VMEM((HD, 4 * TILE), jnp.float32),
            pltpu.VMEM((4 * TILE, HD), bf16),
            pltpu.VMEM((ROWS, WIDTH), bf16),
            dma((5,)), dma((5,)), dma((5,)), dma((5,)),
            dma((4,)), dma((4,)), dma((4,)), dma((4,)), dma((4,)), dma((4,)),
            dma((6,)), dma((6,)), dma((6, 4)), dma((6, 4)), dma((8, 6)), dma((8, 6)), dma((16,)), dma((16,)), dma((8,)),
        ],
        compiler_params=pltpu.CompilerParams(
            collective_id=0, has_side_effects=True, vmem_limit_bytes=56 << 20
        ),
    )(
        lengths,
        hidden_states[0],
        jnp.transpose(modulation, (1, 0, 2)),
        jnp.transpose(w_qkv, (1, 0, 2)),
        w_out,
    )
    return updated[None]


def solution(mesh):
    placed = (
        P("wrow", ("patch", "wcol"), None),
        P("wrow", None, None),
        P("wrow", None, "wcol"),
        P("wcol", "wrow"),
        P("wrow"),
    )
    return jax.shard_map(
        body,
        mesh=mesh,
        in_specs=placed,
        out_specs=P("wrow", ("patch", "wcol"), None),
        check_vma=False,
    )
```
